32 devices in a mesh: heads: 2 (over core), blk: 16 (over z, y, x).
Axes of the slice: x: 2, y: 2, z: 4, core: 2. Of those that a mesh axis runs over, the one named last changes fastest.
Arguments:
- queries: bfloat16 [3072, 4096], P('blk', 'heads'), may hold values from -8 to 8
- keys: bfloat16 [3072, 4096], P('blk', 'heads'), may hold values from -6 to 6
- values: bfloat16 [3072, 4096], P('blk', 'heads'), may hold values from -24 to 24
- prefix_keys: bfloat16 [1024, 4096], P('blk', 'heads'), may hold values from -8 to 8
- prefix_values: bfloat16 [1024, 4096], P('blk', 'heads'), may hold values from -24 to 24
- lengths: int32 [24], replicated, may hold values from 1 to 224, 3072 in all
- groups: int32 [24], replicated, may hold values from 0 to 3, as said below
- out_weight: bfloat16 [4096, 4096], P('heads'), may hold values from -0.09375 to 0.09375
Outputs:
- attn_branch: bfloat16 [3072, 4096], P('blk', 'heads')
The draws below stay inside these ranges and needn't reach their ends.
Inputs may be any that keep to these rules, and one draw needn't show every extreme that they name: Each of the 4 groups holds 6 requests. The lengths sum to 3072; the longest is 224.
All inputs are finite; a program needn't handle non-finite values.
Results may differ from the reference program's by a relative error of at most 0.019.
Values may be sent and summed in bfloat16 or wider, within the bound.
A program may use at most 128 MiB of HBM per device.

```python
import math
import jax
import jax.numpy as jnp
import numpy as np
from jax import lax

D = 4096
HEADS = 32
HD = 128
ROT = 32
GROUPS = 4
MOST = 224
TOKENS = 3072
REQUESTS = 24
PREFIX = 256


def draw_queries(key, part):
    inner = jax.random.fold_in(key, 21)
    base = jnp.clip(1.5 * jax.random.normal(inner, (TOKENS, HEADS, HD), jnp.float32), -8.0, 8.0)
    return base.reshape(TOKENS, D).astype(jnp.bfloat16)


def draw_prefix_keys(key, part):
    inner = jax.random.fold_in(key, 23)
    rows_all = GROUPS * PREFIX
    base = jnp.clip(jax.random.normal(inner, (rows_all, HEADS, HD), jnp.float32), -8.0, 8.0)
    return base.reshape(rows_all, D).astype(jnp.bfloat16)


def draw_groups(key, part):
    order = jax.random.permutation(jax.random.fold_in(key, 31), REQUESTS)
    return (order % GROUPS).astype(jnp.int32)


def levels(own_key, dims, shards, smallest, largest):
    def one(dim, blocks):
        heights = jax.random.uniform(jax.random.fold_in(jax.random.fold_in(own_key, 6), dim), (blocks,), jnp.float32, smallest / len(shards), largest / len(shards))
        return jnp.repeat(jnp.exp(heights), dims[dim] // blocks).reshape((-1,) + (1,) * (len(dims) - dim - 1))

    level = one(*shards[0])
    for cut in shards[1:]:
        level = level * one(*cut)
    return level


def length_profile(count, total, bound, skew):
    weights = [(1 << 20) // math.isqrt(grade ** skew) + 1 for grade in range(2, count + 1)]
    rest, counts = total - bound - (count - 1), [1] * (count - 1)
    while rest > 0:
        movable = [i for i in range(count - 1) if counts[i] < bound]
        mass, left = sum([weights[i] for i in movable]), rest
        for i in movable:
            extra = min(bound - counts[i], max(1, left * weights[i] // mass), rest)
            counts[i] = counts[i] + extra
            rest = rest - extra
    return np.array([bound] + counts)


def ragged_sizes(stream_key, count, total, bound, lean):
    if count == 2:
        one = jax.random.randint(stream_key, (), max(1, total - bound), min(bound, total - 1) + 1)
        return jnp.stack([one, total - one])
    sizes = jnp.asarray(length_profile(count, total, bound, lean), jnp.int32)
    twos = (count - 1) // 2
    giver, taker = sizes[1:1 + 2 * twos:2], sizes[2:2 + 2 * twos:2]
    room = jnp.minimum(giver - 1, bound - taker)
    shifted = jax.random.randint(jax.random.fold_in(stream_key, 1), (twos,), 0, 1 << 20) % (room + 1)
    sizes = sizes.at[1:1 + 2 * twos:2].set(giver - shifted).at[2:2 + 2 * twos:2].set(taker + shifted)
    return sizes[jax.random.permutation(jax.random.fold_in(stream_key, 2), count)]


def scatter_about(rng, dims, scale, reach, split=(), kind=jnp.bfloat16):
    values = jax.random.normal(rng, dims, jnp.float32) * scale
    if len(split) > 0:
        values = levels(rng, dims, split, -0.22, 0.18) * values
    return jnp.clip(values, min=-reach, max=reach).astype(kind)


def setup_inputs(seed: int = 0) -> dict:
    key_list = jax.random.split(jax.random.key(seed), 9)
    queries = draw_queries(jax.random.fold_in(key_list[8], 71), 0)
    keys = scatter_about(key_list[1], (TOKENS, D), 1.0, 6.0, ((0, 16), (1, 2)))
    values = scatter_about(key_list[2], (TOKENS, D), 4.0, 24.0, ((0, 16), (1, 2)))
    prefix_keys = draw_prefix_keys(jax.random.fold_in(key_list[8], 71), 0)
    prefix_values = scatter_about(key_list[4], (GROUPS * PREFIX, D), 4.0, 24.0, ((0, 16), (1, 2)))
    lengths = ragged_sizes(key_list[5], REQUESTS, TOKENS, MOST, 2).astype(jnp.int32)
    groups = draw_groups(jax.random.fold_in(key_list[8], 71), 0)
    out_weight = scatter_about(key_list[7], (D, D), D ** -0.5, 0.09375, ((0, 2),))
    return dict(queries=queries, keys=keys, values=values, prefix_keys=prefix_keys, prefix_values=prefix_values, lengths=lengths, groups=groups, out_weight=out_weight)


def token_tables(lengths, groups, tok_index, prefix_len):
    ends = jnp.cumsum(lengths).astype(jnp.int32)
    starts = ends - lengths
    inside = (starts[None, :] <= tok_index[:, None]) & (tok_index[:, None] < ends[None, :])
    start_tok = lax.optimization_barrier(jnp.sum(jnp.where(inside, starts[None, :] + 1, 0), axis=1)).astype(jnp.int32) - 1
    group_tok = lax.optimization_barrier(jnp.sum(jnp.where(inside, groups[None, :], 0), axis=1)).astype(jnp.int32)
    position = (prefix_len + tok_index - start_tok).astype(jnp.int32)
    return (start_tok, group_tok, position)

def rotary(field, position):
    half = ROT // 2
    inverse = 10000.0 ** (-(jnp.arange(half, dtype=jnp.float32) * 2.0 / ROT))
    angle = position.astype(jnp.float32)[:, None] * inverse[None, :]
    angle = jnp.concatenate([angle, angle], axis=1)
    cosine = jnp.cos(angle)[:, None, :]
    sine = jnp.sin(angle)[:, None, :]
    front = field[..., :ROT]
    turned = jnp.concatenate([-front[..., half:], front[..., :half]], axis=-1)
    rotated = front * cosine + turned * sine
    return jnp.concatenate([rotated, field[..., ROT:]], axis=-1)

def reference(queries, keys, values, prefix_keys, prefix_values, lengths, groups, out_weight):
    scale = 1.0 / math.sqrt(HD)
    tok_index = jnp.arange(TOKENS, dtype=jnp.int32)
    start_tok, group_tok, position = token_tables(lengths, groups, tok_index, PREFIX)
    q_rot = rotary(queries.reshape(TOKENS, HEADS, HD).astype(jnp.float32), position).astype(jnp.bfloat16)
    k_rot = rotary(keys.reshape(TOKENS, HEADS, HD).astype(jnp.float32), position).astype(jnp.bfloat16)
    v_all = values.reshape(TOKENS, HEADS, HD)
    block = math.gcd(128, TOKENS)
    margin = block * ((MOST - 1 + block - 1) // block)
    k_pad = jnp.concatenate([jnp.zeros((margin, HEADS, HD), jnp.bfloat16), k_rot], axis=0)
    v_pad = jnp.concatenate([jnp.zeros((margin, HEADS, HD), jnp.bfloat16), v_all], axis=0)
    start_pad = jnp.concatenate([jnp.full((margin,), -1, jnp.int32), start_tok], axis=0)
    pre_k = prefix_keys.reshape(GROUPS * PREFIX, HEADS, HD)
    pre_v = prefix_values.reshape(GROUPS * PREFIX, HEADS, HD)
    pre_group = (jnp.arange(GROUPS * PREFIX, dtype=jnp.int32) // PREFIX).astype(jnp.int32)

    def one_block(number):
        first = (number * block).astype(jnp.int32)
        q_blk = lax.dynamic_slice_in_dim(q_rot, first, block, 0)
        q_idx = first + jnp.arange(block, dtype=jnp.int32)
        q_start = lax.dynamic_slice_in_dim(start_tok, first, block, 0)
        q_group = lax.dynamic_slice_in_dim(group_tok, first, block, 0)
        w_k = lax.dynamic_slice_in_dim(k_pad, first, margin + block, 0)
        w_v = lax.dynamic_slice_in_dim(v_pad, first, margin + block, 0)
        w_start = lax.dynamic_slice_in_dim(start_pad, first, margin + block, 0)
        w_idx = first - margin + jnp.arange(margin + block, dtype=jnp.int32)
        suffix_mask = (w_start[None, :] == q_start[:, None]) & (w_idx[None, :] <= q_idx[:, None])
        prefix_mask = pre_group[None, :] == q_group[:, None]
        mask = jnp.concatenate([prefix_mask, suffix_mask], axis=1)
        all_k = jnp.concatenate([pre_k, w_k], axis=0).astype(jnp.float32)
        all_v = jnp.concatenate([pre_v, w_v], axis=0).astype(jnp.float32)
        score = jnp.einsum('qhd,khd->hqk', q_blk.astype(jnp.float32), all_k) * scale
        score = jnp.where(mask[None], score, -1e+30)
        top = lax.optimization_barrier(jnp.max(score, axis=-1, keepdims=True))
        expo = jnp.exp(score - top)
        total = lax.optimization_barrier(jnp.sum(expo, axis=-1))
        weights = expo.astype(jnp.bfloat16).astype(jnp.float32)
        accum = jnp.einsum('hqk,khd->qhd', weights, all_v)
        attn = accum / jnp.transpose(total)[:, :, None]
        return attn.reshape(block, D).astype(jnp.bfloat16)
    attn = lax.map(one_block, jnp.arange(TOKENS // block, dtype=jnp.int32)).reshape(TOKENS, D)
    return jnp.dot(attn, out_weight, preferred_element_type=jnp.float32).astype(jnp.bfloat16)
```

```python
import functools
import math

import jax
import jax.numpy as jnp
from jax import lax
from jax.experimental import pallas as pl
from jax.experimental.pallas import tpu as pltpu
from jax.sharding import PartitionSpec as P

HD = 128
ROT = 32
GROUPS = 4
MOST = 224
HALO = (MOST - 1 + 15) // 16 * 16
TILE = 256
MESH = pl.DeviceIdType.MESH


def request_tables(lengths, groups, index):
    ends = jnp.cumsum(lengths)
    starts = ends - lengths
    inside = (starts <= index[..., None]) & (index[..., None] < ends)
    start = jnp.sum(jnp.where(inside, starts + 1, 0), axis=-1) - 1
    group = jnp.sum(jnp.where(inside, groups, 0), axis=-1)
    return start, group


def rotary_tables(position):
    half = ROT // 2
    inverse = 10000.0 ** (-(jnp.arange(half, dtype=jnp.float32) * 2.0 / ROT))
    angle = position.astype(jnp.float32)[:, None] * inverse[None, :]
    cosine, sine = jnp.cos(angle), jnp.sin(angle)
    rest = jnp.zeros((position.shape[0], HD - ROT), jnp.float32)
    none = jnp.zeros_like(sine)
    same = jnp.concatenate([cosine, cosine, rest + 1.0], axis=1)
    below = jnp.concatenate([-sine, none, rest], axis=1)
    above = jnp.concatenate([none, sine, rest], axis=1)
    return jnp.stack([same, below, above])


def dot_t(a, b):
    return lax.dot_general(a, b, (((1,), (1,)), ((), ())), preferred_element_type=jnp.float32)


def kernel(
    part, n_line, n_heads,
    q_ref, k_ref, v_ref, pk_ref, pv_ref, rot_ref, qs_ref, qg_ref, ks_ref, w_ref,
    out_ref,
    q_turn, k_turn, q_all, k_all, v_all, pk_all, pv_all, sent, attn, weight, give, take, own,
    pre_s, pre_r, qkv_s, qkv_r, line_s, line_r, halo_s, halo_r, back_s, back_r, sum_s, sum_r, w_sem,
):
    tok, width = q_ref.shape
    cols = width // part
    rows_pre = pk_ref.shape[0]
    n_pre = pk_all.shape[0]
    prefix_len = n_pre // GROUPS
    out_w = out_ref.shape[1]
    blk = lax.axis_index("blk")
    head = lax.axis_index("heads")
    line = blk // part
    member = blk % part
    base = line * part

    fetch = pltpu.make_async_copy(w_ref, weight, w_sem)
    fetch.start()

    barrier = pltpu.get_barrier_semaphore()
    for j in range(1, part):
        pl.semaphore_signal(
            barrier, inc=1, device_id={"blk": base + (member + j) % part}, device_id_type=MESH
        )
    for j in range(1, n_line):
        pl.semaphore_signal(
            barrier, inc=1, device_id={"blk": (line + j) % n_line * part + member},
            device_id_type=MESH,
        )
    for j in range(1, n_heads):
        pl.semaphore_signal(
            barrier, inc=1, device_id={"heads": (head + j) % n_heads}, device_id_type=MESH
        )
    pl.semaphore_wait(barrier, part + n_line + n_heads - 3)

    def columns(m):
        return pl.ds(pl.multiple_of(m * cols, cols), cols)

    def to_plane(src, dst, row, rows, send, recv, j):
        peer = (member + j) % part
        copy = pltpu.make_async_remote_copy(
            src_ref=src.at[:, columns(peer)],
            dst_ref=dst.at[pl.ds(pl.multiple_of(row, 16), rows), :],
            send_sem=send, recv_sem=recv,
            device_id={"blk": base + peer}, device_id_type=MESH,
        )
        copy.start()
        return copy

    pre_row = blk * rows_pre
    pre = [
        to_plane(src, dst, pre_row, rows_pre, pre_s.at[i, j], pre_r.at[i, j], j)
        for i, (src, dst) in enumerate(((pk_ref, pk_all), (pv_ref, pv_all)))
        for j in range(1, part)
    ]
    tok_row = member * tok
    moved = [
        to_plane(v_ref, v_all, HALO + tok_row, tok, qkv_s.at[2, j], qkv_r.at[2, j], j)
        for j in range(1, part)
    ]
    own_pre = pl.ds(pl.multiple_of(pre_row, 16), rows_pre)
    pk_all[own_pre, :] = pk_ref[:, columns(member)]
    pv_all[own_pre, :] = pv_ref[:, columns(member)]

    same, below, above = rot_ref[0], rot_ref[1], rot_ref[2]

    def turn(src, dst):
        for h in range(width // HD):
            at = slice(h * HD, (h + 1) * HD)
            x = src[:, at].astype(jnp.float32)
            y = x * same + pltpu.roll(x, HD - ROT // 2, 1) * below + pltpu.roll(x, ROT // 2, 1) * above
            dst[:, at] = y.astype(jnp.bfloat16)

    turn(k_ref, k_turn)
    moved += [
        to_plane(k_turn, k_all, HALO + tok_row, tok, qkv_s.at[1, j], qkv_r.at[1, j], j)
        for j in range(1, part)
    ]

    for copy in pre:
        copy.wait_recv()
    here = pl.ds(pl.multiple_of(line * (part * rows_pre), 16), part * rows_pre)
    lines = []
    for j in range(1, n_line):
        peer = (line + j) % n_line * part + member
        for i, ref in enumerate((pk_all, pv_all)):
            copy = pltpu.make_async_remote_copy(
                src_ref=ref.at[here, :], dst_ref=ref.at[here, :],
                send_sem=line_s.at[i, j], recv_sem=line_r.at[i, j],
                device_id={"blk": peer}, device_id_type=MESH,
            )
            copy.start()
            lines.append(copy)

    turn(q_ref, q_turn)
    moved_q = [
        to_plane(q_turn, q_all, tok_row, tok, qkv_s.at[0, j], qkv_r.at[0, j], j)
        for j in range(1, part)
    ]
    q_all[pl.ds(pl.multiple_of(tok_row, 16), tok), :] = q_turn[:, columns(member)]
    own_kv = pl.ds(pl.multiple_of(HALO + tok_row, 16), tok)
    k_all[own_kv, :] = k_turn[:, columns(member)]
    v_all[own_kv, :] = v_ref[:, columns(member)]

    for copy in moved:
        copy.wait_recv()
    halos = [
        pltpu.make_async_remote_copy(
            src_ref=ref.at[pl.ds(part * tok, HALO), :], dst_ref=ref.at[pl.ds(0, HALO), :],
            send_sem=halo_s.at[i], recv_sem=halo_r.at[i],
            device_id={"blk": (line + 1) % n_line * part + member}, device_id_type=MESH,
        )
        for i, ref in enumerate((k_all, v_all))
    ]

    @pl.when(line < n_line - 1)
    def _():
        for copy in halos:
            copy.start()

    @pl.when(line == 0)
    def _():
        k_all[pl.ds(0, HALO), :] = jnp.zeros((HALO, cols), jnp.bfloat16)
        v_all[pl.ds(0, HALO), :] = jnp.zeros((HALO, cols), jnp.bfloat16)

    for copy in moved_q:
        copy.wait_recv()

    @pl.when(line > 0)
    def _():
        for copy in halos:
            copy.wait_recv()

    for copy in lines:
        copy.wait_recv()

    span = HALO + tok
    factor = math.log2(math.e) / math.sqrt(HD)
    later = lax.broadcasted_iota(jnp.int32, (tok, span), 1) - HALO <= lax.broadcasted_iota(
        jnp.int32, (tok, span), 0
    )

    def send_back(step):
        peer = (member + step) % part
        row = pl.ds(pl.multiple_of(peer * tok, 16), tok)
        return pltpu.make_async_remote_copy(
            src_ref=sent.at[row, :], dst_ref=attn.at[:, columns(member)],
            send_sem=back_s.at[step], recv_sem=back_r.at[step],
            device_id={"blk": base + peer}, device_id_type=MESH,
        )

    def block(step, carry):
        b = (member + step) % part
        row = pl.ds(pl.multiple_of(b * tok, 16), tok)
        window = pl.ds(pl.multiple_of(b * tok, 16), span)
        group = qg_ref[row, :]
        allowed = (ks_ref[b] == qs_ref[row, :]) & later
        for h in range(cols // HD):
            at = slice(h * HD, (h + 1) * HD)
            q = q_all[row, at]
            near = jnp.where(allowed, dot_t(q, k_all[window, at]), -1e30)
            far = dot_t(q, pk_all[0:prefix_len, at])
            for g in range(1, GROUPS):
                far = jnp.where(
                    group == g, dot_t(q, pk_all[g * prefix_len:(g + 1) * prefix_len, at]), far
                )
            top = jnp.maximum(
                jnp.max(near, axis=1, keepdims=True), jnp.max(far, axis=1, keepdims=True)
            )
            e_near = jnp.exp2((near - top) * factor)
            e_far = jnp.exp2((far - top) * factor)
            total = jnp.sum(e_near, axis=1, keepdims=True) + jnp.sum(e_far, axis=1, keepdims=True)
            acc = jnp.dot(
                e_near.astype(jnp.bfloat16), v_all[window, at], preferred_element_type=jnp.float32
            )
            for g in range(GROUPS):
                acc += jnp.dot(
                    jnp.where(group == g, e_far, 0.0).astype(jnp.bfloat16),
                    pv_all[g * prefix_len:(g + 1) * prefix_len, at],
                    preferred_element_type=jnp.float32,
                )
            sent[row, at] = (acc / total).astype(jnp.bfloat16)

        @pl.when(step < part)
        def _():
            send_back(step).start()

        return carry

    lax.fori_loop(1, part + 1, block, 0)
    attn[:, columns(member)] = sent[pl.ds(pl.multiple_of(tok_row, 16), tok), :]
    for step in range(1, part):
        send_back(step).wait_recv()
    fetch.wait()

    def project(first, t):
        at = pl.ds(pl.multiple_of(first + t * TILE, TILE), TILE)
        return jnp.dot(attn[...], weight[:, at], preferred_element_type=jnp.float32)

    sums = []
    for j in range(1, n_heads):
        peer = (head + j) % n_heads

        @pl.loop(0, out_w // TILE)
        def _(t):
            at = pl.ds(pl.multiple_of(t * TILE, TILE), TILE)
            give[j - 1, :, at] = project(peer * out_w, t).astype(jnp.bfloat16)

        copy = pltpu.make_async_remote_copy(
            src_ref=give.at[j - 1], dst_ref=take.at[j - 1],
            send_sem=sum_s.at[j], recv_sem=sum_r.at[j],
            device_id={"heads": peer}, device_id_type=MESH,
        )
        copy.start()
        sums.append(copy)

    @pl.loop(0, out_w // TILE)
    def _(t):
        at = pl.ds(pl.multiple_of(t * TILE, TILE), TILE)
        own[:, at] = project(head * out_w, t)

    for copy in sums:
        copy.wait_recv()

    @pl.loop(0, out_w // TILE)
    def _(t):
        at = pl.ds(pl.multiple_of(t * TILE, TILE), TILE)
        whole = own[:, at]
        for j in range(1, n_heads):
            whole += take[j - 1, :, at].astype(jnp.float32)
        out_ref[:, at] = whole.astype(jnp.bfloat16)

    for copy in pre + moved + lines + moved_q + sums:
        copy.wait_send()
    for step in range(1, part):
        send_back(step).wait_send()

    @pl.when(line < n_line - 1)
    def _():
        for copy in halos:
            copy.wait_send()


def body(queries, keys, values, prefix_keys, prefix_values, lengths, groups, out_weight):
    tok, width = queries.shape
    rows_pre = prefix_keys.shape[0]
    n_blk = lax.axis_size("blk")
    n_heads = lax.axis_size("heads")
    part = math.gcd(4, math.gcd(width // HD, n_blk))
    n_line = n_blk // part
    cols = width // part
    n_pre = rows_pre * n_blk
    out_w = out_weight.shape[1] // n_heads
    blk = lax.axis_index("blk")
    first = blk // part * (part * tok)
    plane = first + jnp.arange(part * tok, dtype=jnp.int32)
    start, group = request_tables(lengths, groups, plane)
    window = (
        first - HALO
        + jnp.arange(part, dtype=jnp.int32)[:, None, None] * tok
        + jnp.arange(HALO + tok, dtype=jnp.int32)[None, None, :]
    )
    near_start = request_tables(lengths, groups, window)[0]
    mine = blk * tok + jnp.arange(tok, dtype=jnp.int32)
    position = n_pre // GROUPS + mine - request_tables(lengths, groups, mine)[0]
    tables = rotary_tables(position)
    vmem = pl.BlockSpec(memory_space=pltpu.VMEM)
    bf = jnp.bfloat16
    dma = pltpu.SemaphoreType.DMA
    return pl.pallas_call(
        functools.partial(kernel, part, n_line, n_heads),
        out_shape=jax.ShapeDtypeStruct((tok, out_w), bf),
        in_specs=[vmem] * 9 + [pl.BlockSpec(memory_space=pl.ANY)],
        out_specs=vmem,
        scratch_shapes=[
            pltpu.VMEM((tok, width), bf),
            pltpu.VMEM((tok, width), bf),
            pltpu.VMEM((part * tok, cols), bf),
            pltpu.VMEM((HALO + part * tok, cols), bf),
            pltpu.VMEM((HALO + part * tok, cols), bf),
            pltpu.VMEM((n_pre, cols), bf),
            pltpu.VMEM((n_pre, cols), bf),
            pltpu.VMEM((part * tok, cols), bf),
            pltpu.VMEM((tok, width), bf),
            pltpu.VMEM(out_weight.shape, bf),
            pltpu.VMEM((n_heads - 1, tok, out_w), bf),
            pltpu.VMEM((n_heads - 1, tok, out_w), bf),
            pltpu.VMEM((tok, out_w), jnp.float32),
            dma((2, part)), dma((2, part)),
            dma((3, part)), dma((3, part)),
            dma((2, n_line)), dma((2, n_line)),
            dma((2,)), dma((2,)),
            dma((part,)), dma((part,)),
            dma((n_heads,)), dma((n_heads,)),
            dma,
        ],
        compiler_params=pltpu.CompilerParams(
            collective_id=0, has_side_effects=True, vmem_limit_bytes=56 << 20
        ),
    )(
        queries, keys, values, prefix_keys, prefix_values, tables,
        start[:, None], group[:, None], near_start, out_weight,
    )


def solution(mesh):
    placed = (
        P("blk", "heads"),
        P("blk", "heads"),
        P("blk", "heads"),
        P("blk", "heads"),
        P("blk", "heads"),
        P(),
        P(),
        P("heads", None),
    )
    return jax.shard_map(
        body, mesh=mesh, in_specs=placed, out_specs=P("blk", "heads"), check_vma=False
    )
```

```python
import functools
import math

import jax
import jax.numpy as jnp
import numpy as np
from jax import lax
from jax.experimental import pallas as pl
from jax.experimental.pallas import tpu as pltpu
from jax.sharding import PartitionSpec as P

HD = 128
ROT = 32
GROUPS = 4
MOST = 224
HALO = (MOST - 1 + 15) // 16 * 16
TILE = 256
MESH = pl.DeviceIdType.MESH


def rotary_rates():
    half = ROT // 2
    rates = np.zeros((1, HD), np.float32)
    rates[0, :half] = 10000.0 ** (-(np.arange(half, dtype=np.float32) * np.float32(2.0 / ROT)))
    rates[0, half:ROT] = rates[0, :half]
    return rates


def dot_t(a, b):
    return lax.dot_general(a, b, (((1,), (1,)), ((), ())), preferred_element_type=jnp.float32)


def kernel(
    part, n_line, n_heads,
    len_ref, grp_ref, rate_ref, q_ref, k_ref, v_ref, pk_ref, pv_ref, w_ref,
    own, take,
    q_in, k_in, q_turn, k_turn, q_all, k_all, v_all, pk_all, pv_all, sent, attn, weight, give,
    begin, group_of, near_begin,
    pre_s, pre_r, qkv_s, qkv_r, line_s, line_r, halo_s, halo_r, back_s, back_r, sum_s, sum_r,
    in_sem, own_sem, w_sem,
):
    tok, width = q_ref.shape
    cols = width // part
    rows_pre = pk_ref.shape[0]
    n_pre = pk_all.shape[0]
    prefix_len = n_pre // GROUPS
    out_w = own.shape[1]
    requests = len_ref.shape[0]
    span = HALO + tok
    blk = lax.axis_index("blk")
    head = lax.axis_index("heads")
    line = blk // part
    member = blk % part
    base = line * part

    fetch = pltpu.make_async_copy(w_ref, weight, w_sem)
    loads = [
        pltpu.make_async_copy(k_ref, k_in, in_sem.at[0]),
        pltpu.make_async_copy(q_ref, q_in, in_sem.at[1]),
    ]
    for copy in loads:
        copy.start()

    barrier = pltpu.get_barrier_semaphore()
    for j in range(1, part):
        pl.semaphore_signal(
            barrier, inc=1, device_id={"blk": base + (member + j) % part}, device_id_type=MESH
        )
    for j in range(1, n_line):
        pl.semaphore_signal(
            barrier, inc=1, device_id={"blk": (line + j) % n_line * part + member},
            device_id_type=MESH,
        )
    for j in range(1, n_heads):
        pl.semaphore_signal(
            barrier, inc=1, device_id={"heads": (head + j) % n_heads}, device_id_type=MESH
        )
    pl.semaphore_wait(barrier, part + n_line + n_heads - 3)

    def columns(m):
        return pl.ds(pl.multiple_of(m * cols, cols), cols)

    def to_plane(src, dst, row, rows, send, recv, j):
        peer = (member + j) % part
        copy = pltpu.make_async_remote_copy(
            src_ref=src.at[:, columns(peer)],
            dst_ref=dst.at[pl.ds(pl.multiple_of(row, 16), rows), :],
            send_sem=send, recv_sem=recv,
            device_id={"blk": base + peer}, device_id_type=MESH,
        )
        copy.start()
        return copy

    pre_row = blk * rows_pre
    pre = [
        to_plane(src, dst, pre_row, rows_pre, pre_s.at[i, j], pre_r.at[i, j], j)
        for i, (src, dst) in enumerate(((pk_ref, pk_all), (pv_ref, pv_all)))
        for j in range(1, part)
    ]
    tok_row = member * tok
    moved = [
        to_plane(v_ref, v_all, HALO + tok_row, tok, qkv_s.at[2, j], qkv_r.at[2, j], j)
        for j in range(1, part)
    ]
    own_pre = pl.ds(pl.multiple_of(pre_row, 16), rows_pre)
    own_row = pl.ds(pl.multiple_of(tok_row, 16), tok)
    own_kv = pl.ds(pl.multiple_of(HALO + tok_row, 16), tok)
    local = [
        pltpu.make_async_copy(pk_ref.at[:, columns(member)], pk_all.at[own_pre, :], own_sem.at[0]),
        pltpu.make_async_copy(pv_ref.at[:, columns(member)], pv_all.at[own_pre, :], own_sem.at[1]),
        pltpu.make_async_copy(v_ref.at[:, columns(member)], v_all.at[own_kv, :], own_sem.at[2]),
    ]
    for copy in local:
        copy.start()
    fetch.start()

    def request(r, state, queries, near):
        start, begins, owners, nears = state
        length = len_ref[r]
        end = start + length
        inside = (queries >= start) & (queries < end)
        begins = jnp.where(inside, start + 1, begins)
        if owners is not None:
            owners = jnp.where(inside, grp_ref[r], owners)
        if nears is not None:
            nears = jnp.where((near >= start) & (near < end), start + 1, nears)
        return end, begins, owners, nears

    index = blk * tok + lax.broadcasted_iota(jnp.int32, (tok, 1), 0)
    zero = jnp.zeros((tok, 1), jnp.int32)
    mine = lax.fori_loop(
        0, requests, lambda r, state: request(r, state, index, None),
        (jnp.int32(0), zero, None, None),
    )[1]
    position = prefix_len + index + 1 - mine
    angle = position.astype(jnp.float32) * rate_ref[...]
    lane = lax.broadcasted_iota(jnp.int32, (tok, HD), 1)
    same, sine = jnp.cos(angle), jnp.sin(angle)
    below = jnp.where(lane < ROT // 2, -sine, 0.0)
    above = jnp.where(lane < ROT // 2, 0.0, sine)

    def turn(src, dst):
        for h in range(width // HD):
            at = slice(h * HD, (h + 1) * HD)
            x = src[:, at].astype(jnp.float32)
            y = x * same + pltpu.roll(x, HD - ROT // 2, 1) * below + pltpu.roll(x, ROT // 2, 1) * above
            dst[:, at] = y.astype(jnp.bfloat16)

    loads[0].wait()
    turn(k_in, k_turn)
    moved += [
        to_plane(k_turn, k_all, HALO + tok_row, tok, qkv_s.at[1, j], qkv_r.at[1, j], j)
        for j in range(1, part)
    ]

    for copy in pre:
        copy.wait_recv()
    for copy in local[:2]:
        copy.wait()
    shard = part * rows_pre

    def hop(sign, i, d):
        ref = (pk_all, pv_all)[i]
        side = (sign + 1) // 2
        away = lax.rem(line - sign * (d - 1) + n_line, n_line)
        rows = pl.ds(pl.multiple_of(away * shard, 16), shard)
        return pltpu.make_async_remote_copy(
            src_ref=ref.at[rows, :], dst_ref=ref.at[rows, :],
            send_sem=line_s.at[side, i, d], recv_sem=line_r.at[side, i, d],
            device_id={"blk": lax.rem(line + sign + n_line, n_line) * part + member},
            device_id_type=MESH,
        )

    def sends(sign, d):
        if sign > 0:
            return (line >= d - 1) & (line < n_line - 1)
        return (line < n_line - d + 1) & (line > 0)

    def receives(sign, d):
        return line >= d if sign > 0 else line < n_line - d

    def forward(d):
        for i in range(2):
            for sign in (1, -1):
                if d > 1:
                    @pl.when(receives(sign, d - 1))
                    def _():
                        hop(sign, i, d - 1).wait_recv()

                if d < n_line:
                    @pl.when(sends(sign, d))
                    def _():
                        hop(sign, i, d).start()

    forward(1)
    loads[1].wait()
    turn(q_in, q_turn)
    moved_q = [
        to_plane(q_turn, q_all, tok_row, tok, qkv_s.at[0, j], qkv_r.at[0, j], j)
        for j in range(1, part)
    ]
    q_all[own_row, :] = q_turn[:, columns(member)]
    k_all[own_kv, :] = k_turn[:, columns(member)]
    local[2].wait()
    if n_line > 1:
        forward(2)

    for copy in moved:
        copy.wait_recv()
    halos = [
        pltpu.make_async_remote_copy(
            src_ref=ref.at[pl.ds(part * tok, HALO), :], dst_ref=ref.at[pl.ds(0, HALO), :],
            send_sem=halo_s.at[i], recv_sem=halo_r.at[i],
            device_id={"blk": (line + 1) % n_line * part + member}, device_id_type=MESH,
        )
        for i, ref in enumerate((k_all, v_all))
    ]

    @pl.when(line < n_line - 1)
    def _():
        for copy in halos:
            copy.start()

    @pl.when(line == 0)
    def _():
        k_all[pl.ds(0, HALO), :] = jnp.zeros((HALO, cols), jnp.bfloat16)
        v_all[pl.ds(0, HALO), :] = jnp.zeros((HALO, cols), jnp.bfloat16)

    for d in range(3, n_line + 1):
        forward(d)

    def table(b, carry):
        queries = (line * part + b) * tok + lax.broadcasted_iota(jnp.int32, (tok, 1), 0)
        near = (line * part + b) * tok - HALO + lax.broadcasted_iota(jnp.int32, (1, span), 1)
        _, begins, owners, nears = lax.fori_loop(
            0, requests, lambda r, state: request(r, state, queries, near),
            (jnp.int32(0), zero, zero, jnp.zeros((1, span), jnp.int32)),
        )
        row = pl.ds(pl.multiple_of(b * tok, 16), tok)
        begin[row, :] = begins
        group_of[row, :] = owners
        near_begin[b] = nears
        return carry

    lax.fori_loop(0, part, table, 0)

    for copy in moved_q:
        copy.wait_recv()

    @pl.when(line > 0)
    def _():
        for copy in halos:
            copy.wait_recv()

    factor = math.log2(math.e) / math.sqrt(HD)
    later = lax.broadcasted_iota(jnp.int32, (tok, span), 1) - HALO <= lax.broadcasted_iota(
        jnp.int32, (tok, span), 0
    )

    def send_back(step):
        peer = (member + step) % part
        row = pl.ds(pl.multiple_of(peer * tok, 16), tok)
        return pltpu.make_async_remote_copy(
            src_ref=sent.at[row, :], dst_ref=attn.at[:, columns(member)],
            send_sem=back_s.at[step], recv_sem=back_r.at[step],
            device_id={"blk": base + peer}, device_id_type=MESH,
        )

    def block(step, carry):
        b = (member + step) % part
        row = pl.ds(pl.multiple_of(b * tok, 16), tok)
        window = pl.ds(pl.multiple_of(b * tok, 16), span)
        group = group_of[row, :]
        allowed = (near_begin[b] == begin[row, :]) & later
        for h in range(cols // HD):
            at = slice(h * HD, (h + 1) * HD)
            q = q_all[row, at]
            near = jnp.where(allowed, dot_t(q, k_all[window, at]), -1e30)
            far = dot_t(q, pk_all[0:prefix_len, at])
            for g in range(1, GROUPS):
                far = jnp.where(
                    group == g, dot_t(q, pk_all[g * prefix_len:(g + 1) * prefix_len, at]), far
                )
            top = jnp.maximum(
                jnp.max(near, axis=1, keepdims=True), jnp.max(far, axis=1, keepdims=True)
            )
            e_near = jnp.exp2((near - top) * factor)
            e_far = jnp.exp2((far - top) * factor)
            total = jnp.sum(e_near, axis=1, keepdims=True) + jnp.sum(e_far, axis=1, keepdims=True)
            acc = jnp.dot(
                e_near.astype(jnp.bfloat16), v_all[window, at], preferred_element_type=jnp.float32
            )
            for g in range(GROUPS):
                acc += jnp.dot(
                    jnp.where(group == g, e_far, 0.0).astype(jnp.bfloat16),
                    pv_all[g * prefix_len:(g + 1) * prefix_len, at],
                    preferred_element_type=jnp.float32,
                )
            sent[row, at] = (acc / total).astype(jnp.bfloat16)

        @pl.when(step < part)
        def _():
            send_back(step).start()

        return carry

    lax.fori_loop(1, part + 1, block, 0)
    attn[:, columns(member)] = sent[pl.ds(pl.multiple_of(tok_row, 16), tok), :]
    for step in range(1, part):
        send_back(step).wait_recv()
    fetch.wait()

    def project(first, t):
        at = pl.ds(pl.multiple_of(first + t * TILE, TILE), TILE)
        return jnp.dot(attn[...], weight[:, at], preferred_element_type=jnp.float32)

    sums = []
    for j in range(1, n_heads):
        peer = (head + j) % n_heads

        @pl.loop(0, out_w // TILE)
        def _(t):
            at = pl.ds(pl.multiple_of(t * TILE, TILE), TILE)
            give[j - 1, :, at] = project(peer * out_w, t).astype(jnp.bfloat16)

        copy = pltpu.make_async_remote_copy(
            src_ref=give.at[j - 1], dst_ref=take.at[j - 1],
            send_sem=sum_s.at[j], recv_sem=sum_r.at[j],
            device_id={"heads": peer}, device_id_type=MESH,
        )
        copy.start()
        sums.append(copy)

    @pl.loop(0, out_w // TILE)
    def _(t):
        at = pl.ds(pl.multiple_of(t * TILE, TILE), TILE)
        own[:, at] = project(head * out_w, t).astype(jnp.bfloat16)

    for copy in sums:
        copy.wait_recv()

    for copy in pre + moved + moved_q + sums:
        copy.wait_send()
    for d in range(1, n_line):
        for i in range(2):
            for sign in (1, -1):
                @pl.when(sends(sign, d))
                def _():
                    hop(sign, i, d).wait_send()

    for step in range(1, part):
        send_back(step).wait_send()

    @pl.when(line < n_line - 1)
    def _():
        for copy in halos:
            copy.wait_send()


def body(queries, keys, values, prefix_keys, prefix_values, lengths, groups, out_weight):
    tok, width = queries.shape
    rows_pre = prefix_keys.shape[0]
    n_blk = lax.axis_size("blk")
    n_heads = lax.axis_size("heads")
    part = math.gcd(4, math.gcd(width // HD, n_blk))
    n_line = n_blk // part
    cols = width // part
    n_pre = rows_pre * n_blk
    out_w = out_weight.shape[1] // n_heads
    vmem = pl.BlockSpec(memory_space=pltpu.VMEM)
    smem = pl.BlockSpec(memory_space=pltpu.SMEM)
    bf = jnp.bfloat16
    dma = pltpu.SemaphoreType.DMA
    own, others = pl.pallas_call(
        functools.partial(kernel, part, n_line, n_heads),
        out_shape=(
            jax.ShapeDtypeStruct((tok, out_w), bf),
            jax.ShapeDtypeStruct((n_heads - 1, tok, out_w), bf),
        ),
        in_specs=[smem, smem, vmem] + [pl.BlockSpec(memory_space=pl.ANY)] * 6,
        out_specs=(vmem, vmem),
        scratch_shapes=[
            pltpu.VMEM((tok, width), bf),
            pltpu.VMEM((tok, width), bf),
            pltpu.VMEM((tok, width), bf),
            pltpu.VMEM((tok, width), bf),
            pltpu.VMEM((part * tok, cols), bf),
            pltpu.VMEM((HALO + part * tok, cols), bf),
            pltpu.VMEM((HALO + part * tok, cols), bf),
            pltpu.VMEM((n_pre, cols), bf),
            pltpu.VMEM((n_pre, cols), bf),
            pltpu.VMEM((part * tok, cols), bf),
            pltpu.VMEM((tok, width), bf),
            pltpu.VMEM(out_weight.shape, bf),
            pltpu.VMEM((n_heads - 1, tok, out_w), bf),
            pltpu.VMEM((part * tok, 1), jnp.int32),
            pltpu.VMEM((part * tok, 1), jnp.int32),
            pltpu.VMEM((part, 1, HALO + tok), jnp.int32),
            dma((2, part)), dma((2, part)),
            dma((3, part)), dma((3, part)),
            dma((2, 2, n_line)), dma((2, 2, n_line)),
            dma((2,)), dma((2,)),
            dma((part,)), dma((part,)),
            dma((n_heads,)), dma((n_heads,)),
            dma((2,)), dma((3,)), dma,
        ],
        compiler_params=pltpu.CompilerParams(
            collective_id=0, has_side_effects=True, vmem_limit_bytes=56 << 20
        ),
    )(
        lengths, groups, jnp.asarray(rotary_rates()),
        queries, keys, values, prefix_keys, prefix_values, out_weight,
    )
    total = own.astype(jnp.float32)
    for j in range(n_heads - 1):
        total += others[j].astype(jnp.float32)
    return total.astype(bf)


def solution(mesh):
    placed = (
        P("blk", "heads"),
        P("blk", "heads"),
        P("blk", "heads"),
        P("blk", "heads"),
        P("blk", "heads"),
        P(),
        P(),
        P("heads", None),
    )
    return jax.shard_map(
        body, mesh=mesh, in_specs=placed, out_specs=P("blk", "heads"), check_vma=False
    )
```

```python
import functools
import math

import jax
import jax.numpy as jnp
import numpy as np
from jax import lax
from jax.experimental import pallas as pl
from jax.experimental.pallas import tpu as pltpu
from jax.sharding import PartitionSpec as P

HD = 128
ROT = 32
GROUPS = 4
MOST = 224
HALO = (MOST - 1 + 15) // 16 * 16
TILE = 256
MESH = pl.DeviceIdType.MESH


def rotary_rates():
    half = ROT // 2
    rates = np.zeros((1, HD), np.float32)
    rates[0, :half] = 10000.0 ** (-(np.arange(half, dtype=np.float32) * np.float32(2.0 / ROT)))
    rates[0, half:ROT] = rates[0, :half]
    return rates


def dot_t(a, b):
    return lax.dot_general(a, b, (((1,), (1,)), ((), ())), preferred_element_type=jnp.float32)


def kernel(
    part, n_line, n_heads,
    len_ref, grp_ref, rate_ref, q_ref, k_ref, v_ref, pk_ref, pv_ref, w_ref,
    own, take,
    q_in, k_in, q_turn, k_turn, q_all, k_all, v_all, pk_all, pv_all, sent, attn, weight, give, acc,
    begin, group_of, near_begin,
    pre_s, pre_r, qkv_s, qkv_r, line_s, line_r, halo_s, halo_r, back_s, back_r, sum_s, sum_r,
    in_sem, own_sem, w_sem,
):
    tok, width = q_ref.shape
    cols = width // part
    rows_pre = pk_ref.shape[0]
    chunks = len(pk_all)
    n_pre, some = pk_all[0].shape
    prefix_len = n_pre // GROUPS
    out_w = own.shape[1]
    requests = len_ref.shape[0]
    span = HALO + tok
    blk = lax.axis_index("blk")
    head = lax.axis_index("heads")
    line = blk // part
    member = blk % part
    base = line * part

    fetch = [
        pltpu.make_async_copy(
            w_ref.at[pl.ds(m * cols + c * some, some), :],
            weight[c].at[pl.ds(m * some, some), :], w_sem.at[c, m],
        )
        for c in range(chunks)
        for m in range(part)
    ]
    loads = [
        pltpu.make_async_copy(k_ref, k_in, in_sem.at[0]),
        pltpu.make_async_copy(q_ref, q_in, in_sem.at[1]),
    ]
    for copy in loads:
        copy.start()

    barrier = pltpu.get_barrier_semaphore()
    for j in range(1, part):
        pl.semaphore_signal(
            barrier, inc=1, device_id={"blk": base + (member + j) % part}, device_id_type=MESH
        )
    for j in range(1, n_line):
        pl.semaphore_signal(
            barrier, inc=1, device_id={"blk": (line + j) % n_line * part + member},
            device_id_type=MESH,
        )
    for j in range(1, n_heads):
        pl.semaphore_signal(
            barrier, inc=1, device_id={"heads": (head + j) % n_heads}, device_id_type=MESH
        )
    pl.semaphore_wait(barrier, part + n_line + n_heads - 3)

    def columns(m, c):
        return pl.ds(pl.multiple_of(m * cols + c * some, some), some)

    def to_plane(src, dst, c, row, rows, send, recv, j):
        peer = (member + j) % part
        copy = pltpu.make_async_remote_copy(
            src_ref=src.at[:, columns(peer, c)],
            dst_ref=dst[c].at[pl.ds(pl.multiple_of(row, 16), rows), :],
            send_sem=send, recv_sem=recv,
            device_id={"blk": base + peer}, device_id_type=MESH,
        )
        copy.start()
        return copy

    pre_row = blk * rows_pre
    tok_row = member * tok
    pre = [
        [
            to_plane(src, dst, c, pre_row, rows_pre, pre_s.at[i, c, j], pre_r.at[i, c, j], j)
            for i, (src, dst) in enumerate(((pk_ref, pk_all), (pv_ref, pv_all)))
            for j in range(1, part)
        ]
        for c in range(chunks)
    ]

    def move(i, src, dst, first, c):
        return [
            to_plane(src, dst, c, first + tok_row, tok, qkv_s.at[i, c, j], qkv_r.at[i, c, j], j)
            for j in range(1, part)
        ]

    moved = [move(2, v_ref, v_all, HALO, 0)] + [[] for _ in range(chunks - 1)]
    own_pre = pl.ds(pl.multiple_of(pre_row, 16), rows_pre)
    own_row = pl.ds(pl.multiple_of(tok_row, 16), tok)
    own_kv = pl.ds(pl.multiple_of(HALO + tok_row, 16), tok)
    local = [
        pltpu.make_async_copy(
            src.at[:, columns(member, c)], dst[c].at[rows, :], own_sem.at[i, c]
        )
        for i, (src, dst, rows) in enumerate(
            ((pk_ref, pk_all, own_pre), (pv_ref, pv_all, own_pre), (v_ref, v_all, own_kv))
        )
        for c in range(chunks)
    ]
    for copy in local + fetch:
        copy.start()

    def request(r, state, queries, near):
        start, begins, owners, nears = state
        length = len_ref[r]
        end = start + length
        inside = (queries >= start) & (queries < end)
        begins = jnp.where(inside, start + 1, begins)
        if owners is not None:
            owners = jnp.where(inside, grp_ref[r], owners)
        if nears is not None:
            nears = jnp.where((near >= start) & (near < end), start + 1, nears)
        return end, begins, owners, nears

    index = blk * tok + lax.broadcasted_iota(jnp.int32, (tok, 1), 0)
    zero = jnp.zeros((tok, 1), jnp.int32)
    mine = lax.fori_loop(
        0, requests, lambda r, state: request(r, state, index, None),
        (jnp.int32(0), zero, None, None),
    )[1]
    position = prefix_len + index + 1 - mine
    angle = position.astype(jnp.float32) * rate_ref[...]
    lane = lax.broadcasted_iota(jnp.int32, (tok, HD), 1)
    same, sine = jnp.cos(angle), jnp.sin(angle)
    below = jnp.where(lane < ROT // 2, -sine, 0.0)
    above = jnp.where(lane < ROT // 2, 0.0, sine)

    def turn(src, dst):
        for h in range(width // HD):
            at = slice(h * HD, (h + 1) * HD)
            x = src[:, at].astype(jnp.float32)
            y = x * same + pltpu.roll(x, HD - ROT // 2, 1) * below + pltpu.roll(x, ROT // 2, 1) * above
            dst[:, at] = y.astype(jnp.bfloat16)

    loads[0].wait()
    turn(k_in, k_turn)
    moved[0] += move(1, k_turn, k_all, HALO, 0)
    shard = part * rows_pre

    def hop(sign, i, c, d):
        ref = (pk_all, pv_all)[i]
        side = (sign + 1) // 2
        away = lax.rem(line - sign * (d - 1) + n_line, n_line)
        rows = pl.ds(pl.multiple_of(away * shard, 16), shard)
        return pltpu.make_async_remote_copy(
            src_ref=ref[c].at[rows, :], dst_ref=ref[c].at[rows, :],
            send_sem=line_s.at[side, i, c, d], recv_sem=line_r.at[side, i, c, d],
            device_id={"blk": lax.rem(line + sign + n_line, n_line) * part + member},
            device_id_type=MESH,
        )

    def sends(sign, d):
        if sign > 0:
            return (line >= d - 1) & (line < n_line - 1)
        return (line < n_line - d + 1) & (line > 0)

    def receives(sign, d):
        return line >= d if sign > 0 else line < n_line - d

    def forward(c, d):
        for i in range(2):
            for sign in (1, -1):
                if d > 1:
                    @pl.when(receives(sign, d - 1))
                    def _():
                        hop(sign, i, c, d - 1).wait_recv()

                if d < n_line:
                    @pl.when(sends(sign, d))
                    def _():
                        hop(sign, i, c, d).start()

    for copy in local:
        copy.wait()
    for copy in pre[0]:
        copy.wait_recv()
    forward(0, 1)
    loads[1].wait()
    turn(q_in, q_turn)
    moved_q = [move(0, q_turn, q_all, 0, 0)]
    for c in range(1, chunks):
        moved[c] += move(2, v_ref, v_all, HALO, c)
        moved[c] += move(1, k_turn, k_all, HALO, c)
        moved_q.append(move(0, q_turn, q_all, 0, c))
    for c in range(chunks):
        q_all[c][own_row, :] = q_turn[:, columns(member, c)]
        k_all[c][own_kv, :] = k_turn[:, columns(member, c)]

    halos = [
        [
            pltpu.make_async_remote_copy(
                src_ref=ref[c].at[pl.ds(part * tok, HALO), :],
                dst_ref=ref[c].at[pl.ds(0, HALO), :],
                send_sem=halo_s.at[i, c], recv_sem=halo_r.at[i, c],
                device_id={"blk": (line + 1) % n_line * part + member}, device_id_type=MESH,
            )
            for i, ref in enumerate((k_all, v_all))
        ]
        for c in range(chunks)
    ]

    def send_halo(c):
        for copy in moved[c]:
            copy.wait_recv()

        @pl.when(line < n_line - 1)
        def _():
            for copy in halos[c]:
                copy.start()

        @pl.when(line == 0)
        def _():
            k_all[c][pl.ds(0, HALO), :] = jnp.zeros((HALO, some), jnp.bfloat16)
            v_all[c][pl.ds(0, HALO), :] = jnp.zeros((HALO, some), jnp.bfloat16)

    def arrive(c):
        for copy in moved_q[c]:
            copy.wait_recv()

        @pl.when(line > 0)
        def _():
            for copy in halos[c]:
                copy.wait_recv()

    def table(b, carry):
        queries = (line * part + b) * tok + lax.broadcasted_iota(jnp.int32, (tok, 1), 0)
        near = (line * part + b) * tok - HALO + lax.broadcasted_iota(jnp.int32, (1, span), 1)
        _, begins, owners, nears = lax.fori_loop(
            0, requests, lambda r, state: request(r, state, queries, near),
            (jnp.int32(0), zero, zero, jnp.zeros((1, span), jnp.int32)),
        )
        row = pl.ds(pl.multiple_of(b * tok, 16), tok)
        begin[row, :] = begins
        group_of[row, :] = owners
        near_begin[b] = nears
        return carry

    factor = math.log2(math.e) / math.sqrt(HD)
    later = lax.broadcasted_iota(jnp.int32, (tok, span), 1) - HALO <= lax.broadcasted_iota(
        jnp.int32, (tok, span), 0
    )

    def send_back(c, step):
        peer = (member + step) % part
        row = pl.ds(pl.multiple_of(peer * tok, 16), tok)
        return pltpu.make_async_remote_copy(
            src_ref=sent[c].at[row, :],
            dst_ref=attn[c].at[:, pl.ds(pl.multiple_of(member * some, some), some)],
            send_sem=back_s.at[c, step], recv_sem=back_r.at[c, step],
            device_id={"blk": base + peer}, device_id_type=MESH,
        )

    def block(c, step, carry):
        b = (member + step) % part
        row = pl.ds(pl.multiple_of(b * tok, 16), tok)
        window = pl.ds(pl.multiple_of(b * tok, 16), span)
        group = group_of[row, :]
        allowed = (near_begin[b] == begin[row, :]) & later
        for h in range(some // HD):
            at = slice(h * HD, (h + 1) * HD)
            q = q_all[c][row, at]
            near = jnp.where(allowed, dot_t(q, k_all[c][window, at]), -1e30)
            far = dot_t(q, pk_all[c][0:prefix_len, at])
            for g in range(1, GROUPS):
                far = jnp.where(
                    group == g, dot_t(q, pk_all[c][g * prefix_len:(g + 1) * prefix_len, at]), far
                )
            top = jnp.maximum(
                jnp.max(near, axis=1, keepdims=True), jnp.max(far, axis=1, keepdims=True)
            )
            e_near = jnp.exp2((near - top) * factor)
            e_far = jnp.exp2((far - top) * factor)
            total = jnp.sum(e_near, axis=1, keepdims=True) + jnp.sum(e_far, axis=1, keepdims=True)
            acc = jnp.dot(
                e_near.astype(jnp.bfloat16), v_all[c][window, at], preferred_element_type=jnp.float32
            )
            for g in range(GROUPS):
                acc += jnp.dot(
                    jnp.where(group == g, e_far, 0.0).astype(jnp.bfloat16),
                    pv_all[c][g * prefix_len:(g + 1) * prefix_len, at],
                    preferred_element_type=jnp.float32,
                )
            sent[c][row, at] = (acc / total).astype(jnp.bfloat16)

        @pl.when(step < part)
        def _():
            send_back(c, step).start()

        return carry

    def attend(c):
        lax.fori_loop(1, part + 1, functools.partial(block, c), 0)
        attn[c][:, pl.ds(pl.multiple_of(member * some, some), some)] = sent[c][own_row, :]

    def returned(c):
        for step in range(1, part):
            send_back(c, step).wait_recv()
        for copy in fetch[c * part:(c + 1) * part]:
            copy.wait()

    def project(c, at):
        return jnp.dot(attn[c][...], weight[c][:, at], preferred_element_type=jnp.float32)

    def tile(first, t):
        return pl.ds(pl.multiple_of(first + t * TILE, TILE), TILE)

    def gather(c):
        for d in range(2, n_line + 1):
            forward(c, d)
            if d == 2 and c + 1 < chunks:
                for copy in pre[c + 1]:
                    copy.wait_recv()
                forward(c + 1, 1)
            if d == 2 or n_line == 2:
                send_halo(c)
                if c == 0:
                    lax.fori_loop(0, part, table, 0)

    gather(0)
    arrive(0)
    attend(0)
    for c in range(1, chunks):
        gather(c)
        returned(c - 1)

        @pl.loop(0, n_heads * out_w // TILE)
        def _(t):
            at = tile(0, t)
            if c == 1:
                acc[:, at] = project(c - 1, at)
            else:
                acc[:, at] += project(c - 1, at)

        arrive(c)
        attend(c)
    returned(chunks - 1)

    def final(at):
        value = project(chunks - 1, at)
        return value + acc[:, at] if chunks > 1 else value

    sums = []
    for j in range(1, n_heads):
        peer = (head + j) % n_heads

        @pl.loop(0, out_w // TILE)
        def _(t):
            give[j - 1, :, tile(0, t)] = final(tile(peer * out_w, t)).astype(jnp.bfloat16)

        copy = pltpu.make_async_remote_copy(
            src_ref=give.at[j - 1], dst_ref=take.at[j - 1],
            send_sem=sum_s.at[j], recv_sem=sum_r.at[j],
            device_id={"heads": peer}, device_id_type=MESH,
        )
        copy.start()
        sums.append(copy)

    @pl.loop(0, out_w // TILE)
    def _(t):
        own[:, tile(0, t)] = final(tile(head * out_w, t)).astype(jnp.bfloat16)

    for copy in sums:
        copy.wait_recv()

    for copy in sum(pre + moved + moved_q, []) + sums:
        copy.wait_send()
    for c in range(chunks):
        for d in range(1, n_line):
            for i in range(2):
                for sign in (1, -1):
                    @pl.when(sends(sign, d))
                    def _():
                        hop(sign, i, c, d).wait_send()

        for step in range(1, part):
            send_back(c, step).wait_send()

        @pl.when(line < n_line - 1)
        def _():
            for copy in halos[c]:
                copy.wait_send()


def body(queries, keys, values, prefix_keys, prefix_values, lengths, groups, out_weight):
    tok, width = queries.shape
    rows_pre = prefix_keys.shape[0]
    n_blk = lax.axis_size("blk")
    n_heads = lax.axis_size("heads")
    part = math.gcd(4, math.gcd(width // HD, n_blk))
    n_line = n_blk // part
    cols = width // part
    chunks = math.gcd(2, cols // HD)
    some = cols // chunks
    n_pre = rows_pre * n_blk
    out_w = out_weight.shape[1] // n_heads
    vmem = pl.BlockSpec(memory_space=pltpu.VMEM)
    smem = pl.BlockSpec(memory_space=pltpu.SMEM)
    bf = jnp.bfloat16
    dma = pltpu.SemaphoreType.DMA
    own, others = pl.pallas_call(
        functools.partial(kernel, part, n_line, n_heads),
        out_shape=(
            jax.ShapeDtypeStruct((tok, out_w), bf),
            jax.ShapeDtypeStruct((n_heads - 1, tok, out_w), bf),
        ),
        in_specs=[smem, smem, vmem] + [pl.BlockSpec(memory_space=pl.ANY)] * 6,
        out_specs=(vmem, vmem),
        scratch_shapes=[
            pltpu.VMEM((tok, width), bf),
            pltpu.VMEM((tok, width), bf),
            pltpu.VMEM((tok, width), bf),
            pltpu.VMEM((tok, width), bf),
            [pltpu.VMEM((part * tok, some), bf)] * chunks,
            [pltpu.VMEM((HALO + part * tok, some), bf)] * chunks,
            [pltpu.VMEM((HALO + part * tok, some), bf)] * chunks,
            [pltpu.VMEM((n_pre, some), bf)] * chunks,
            [pltpu.VMEM((n_pre, some), bf)] * chunks,
            [pltpu.VMEM((part * tok, some), bf)] * chunks,
            [pltpu.VMEM((tok, width // chunks), bf)] * chunks,
            [pltpu.VMEM((width // chunks, out_weight.shape[1]), bf)] * chunks,
            pltpu.VMEM((n_heads - 1, tok, out_w), bf),
            pltpu.VMEM((tok, out_weight.shape[1]), jnp.float32),
            pltpu.VMEM((part * tok, 1), jnp.int32),
            pltpu.VMEM((part * tok, 1), jnp.int32),
            pltpu.VMEM((part, 1, HALO + tok), jnp.int32),
            dma((2, chunks, part)), dma((2, chunks, part)),
            dma((3, chunks, part)), dma((3, chunks, part)),
            dma((2, 2, chunks, n_line)), dma((2, 2, chunks, n_line)),
            dma((2, chunks)), dma((2, chunks)),
            dma((chunks, part)), dma((chunks, part)),
            dma((n_heads,)), dma((n_heads,)),
            dma((2,)), dma((3, chunks)), dma((chunks, part)),
        ],
        compiler_params=pltpu.CompilerParams(
            collective_id=0, has_side_effects=True, vmem_limit_bytes=56 << 20
        ),
    )(
        lengths, groups, jnp.asarray(rotary_rates()),
        queries, keys, values, prefix_keys, prefix_values, out_weight,
    )
    total = own.astype(jnp.float32)
    for j in range(n_heads - 1):
        total += others[j].astype(jnp.float32)
    return total.astype(bf)


def solution(mesh):
    placed = (
        P("blk", "heads"),
        P("blk", "heads"),
        P("blk", "heads"),
        P("blk", "heads"),
        P("blk", "heads"),
        P(),
        P(),
        P("heads", None),
    )
    return jax.shard_map(
        body, mesh=mesh, in_specs=placed, out_specs=P("blk", "heads"), check_vma=False
    )
```

```python
import functools
import math

import jax
import jax.numpy as jnp
import numpy as np
from jax import lax
from jax.experimental import pallas as pl
from jax.experimental.pallas import tpu as pltpu
from jax.sharding import PartitionSpec as P

HD = 128
ROT = 32
GROUPS = 4
MOST = 224
HALO = (MOST - 1 + 15) // 16 * 16
TILE = 256
MESH = pl.DeviceIdType.MESH


def rotary_rates():
    half = ROT // 2
    rates = np.zeros((1, HD), np.float32)
    rates[0, :half] = 10000.0 ** (-(np.arange(half, dtype=np.float32) * np.float32(2.0 / ROT)))
    rates[0, half:ROT] = rates[0, :half]
    return rates


def dot_t(a, b):
    return lax.dot_general(a, b, (((1,), (1,)), ((), ())), preferred_element_type=jnp.float32)


def kernel(
    part, n_line, n_heads,
    len_ref, grp_ref, rate_ref, q_ref, k_ref, v_ref, pk_ref, pv_ref, w_ref,
    own, take,
    q_in, k_in, q_turn, k_turn, q_all, k_all, v_all, pk_all, pv_all, sent, attn, weight, give, acc,
    begin, group_of, near_begin,
    pre_s, pre_r, qkv_s, qkv_r, line_s, line_r, halo_s, halo_r, back_s, back_r, sum_s, sum_r,
    in_sem, own_sem, w_sem,
):
    tok, width = q_ref.shape
    cols = width // part
    rows_pre = pk_ref.shape[0]
    chunks = len(pk_all)
    n_pre, some = pk_all[0].shape
    prefix_len = n_pre // GROUPS
    out_w = own.shape[1]
    requests = len_ref.shape[0]
    span = HALO + tok
    blk = lax.axis_index("blk")
    head = lax.axis_index("heads")
    line = blk // part
    member = blk % part
    base = line * part

    fetch = [
        pltpu.make_async_copy(
            w_ref.at[pl.ds(m * cols + c * some, some), :],
            weight[c].at[pl.ds(m * some, some), :], w_sem.at[c, m],
        )
        for c in range(chunks)
        for m in range(part)
    ]
    loads = [
        pltpu.make_async_copy(k_ref, k_in, in_sem.at[0]),
        pltpu.make_async_copy(q_ref, q_in, in_sem.at[1]),
    ]
    for copy in loads:
        copy.start()

    barrier = pltpu.get_barrier_semaphore()
    for j in range(1, part):
        pl.semaphore_signal(
            barrier, inc=1, device_id={"blk": base + (member + j) % part}, device_id_type=MESH
        )
    for j in range(1, n_line):
        pl.semaphore_signal(
            barrier, inc=1, device_id={"blk": (line + j) % n_line * part + member},
            device_id_type=MESH,
        )
    for j in range(1, n_heads):
        pl.semaphore_signal(
            barrier, inc=1, device_id={"heads": (head + j) % n_heads}, device_id_type=MESH
        )
    pl.semaphore_wait(barrier, part + n_line + n_heads - 3)

    def columns(m, c):
        return pl.ds(pl.multiple_of(m * cols + c * some, some), some)

    def to_plane(src, dst, c, row, rows, send, recv, j):
        peer = (member + j) % part
        copy = pltpu.make_async_remote_copy(
            src_ref=src.at[:, columns(peer, c)],
            dst_ref=dst[c].at[pl.ds(pl.multiple_of(row, 16), rows), :],
            send_sem=send, recv_sem=recv,
            device_id={"blk": base + peer}, device_id_type=MESH,
        )
        copy.start()
        return copy

    pre_row = blk * rows_pre
    tok_row = member * tok
    pre = [
        [
            to_plane(src, dst, c, pre_row, rows_pre, pre_s.at[i, c, j], pre_r.at[i, c, j], j)
            for i, (src, dst) in enumerate(((pk_ref, pk_all), (pv_ref, pv_all)))
            for j in range(1, part)
        ]
        for c in range(chunks)
    ]

    def move(i, src, dst, first, c):
        return [
            to_plane(src, dst, c, first + tok_row, tok, qkv_s.at[i, c, j], qkv_r.at[i, c, j], j)
            for j in range(1, part)
        ]

    moved = [move(2, v_ref, v_all, HALO, 0)] + [[] for _ in range(chunks - 1)]
    own_pre = pl.ds(pl.multiple_of(pre_row, 16), rows_pre)
    own_row = pl.ds(pl.multiple_of(tok_row, 16), tok)
    own_kv = pl.ds(pl.multiple_of(HALO + tok_row, 16), tok)
    local = [
        pltpu.make_async_copy(
            src.at[:, columns(member, c)], dst[c].at[rows, :], own_sem.at[i, c]
        )
        for i, (src, dst, rows) in enumerate(
            ((pk_ref, pk_all, own_pre), (pv_ref, pv_all, own_pre), (v_ref, v_all, own_kv))
        )
        for c in range(chunks)
    ]
    for copy in local + fetch:
        copy.start()

    def request(r, state, queries, near):
        start, begins, owners, nears = state
        length = len_ref[r]
        end = start + length
        inside = (queries >= start) & (queries < end)
        begins = jnp.where(inside, start + 1, begins)
        if owners is not None:
            owners = jnp.where(inside, grp_ref[r], owners)
        if nears is not None:
            nears = jnp.where((near >= start) & (near < end), start + 1, nears)
        return end, begins, owners, nears

    index = blk * tok + lax.broadcasted_iota(jnp.int32, (tok, 1), 0)
    zero = jnp.zeros((tok, 1), jnp.int32)
    mine = lax.fori_loop(
        0, requests, lambda r, state: request(r, state, index, None),
        (jnp.int32(0), zero, None, None),
    )[1]
    position = prefix_len + index + 1 - mine
    angle = position.astype(jnp.float32) * rate_ref[...]
    lane = lax.broadcasted_iota(jnp.int32, (tok, HD), 1)
    same, sine = jnp.cos(angle), jnp.sin(angle)
    below = jnp.where(lane < ROT // 2, -sine, 0.0)
    above = jnp.where(lane < ROT // 2, 0.0, sine)

    def turn(src, dst):
        for h in range(width // HD):
            at = slice(h * HD, (h + 1) * HD)
            x = src[:, at].astype(jnp.float32)
            y = x * same + pltpu.roll(x, HD - ROT // 2, 1) * below + pltpu.roll(x, ROT // 2, 1) * above
            dst[:, at] = y.astype(jnp.bfloat16)

    loads[0].wait()
    turn(k_in, k_turn)
    moved[0] += move(1, k_turn, k_all, HALO, 0)
    shard = part * rows_pre

    def hop(sign, i, c, d):
        ref = (pk_all, pv_all)[i]
        side = (sign + 1) // 2
        away = lax.rem(line - sign * (d - 1) + n_line, n_line)
        rows = pl.ds(pl.multiple_of(away * shard, 16), shard)
        return pltpu.make_async_remote_copy(
            src_ref=ref[c].at[rows, :], dst_ref=ref[c].at[rows, :],
            send_sem=line_s.at[side, i, c, d], recv_sem=line_r.at[side, i, c, d],
            device_id={"blk": lax.rem(line + sign + n_line, n_line) * part + member},
            device_id_type=MESH,
        )

    def sends(sign, d):
        if sign > 0:
            return (line >= d - 1) & (line < n_line - 1)
        return (line < n_line - d + 1) & (line > 0)

    def receives(sign, d):
        return line >= d if sign > 0 else line < n_line - d

    def forward(c, d):
        for i in range(2):
            for sign in (1, -1):
                if d > 1:
                    @pl.when(receives(sign, d - 1))
                    def _():
                        hop(sign, i, c, d - 1).wait_recv()

                if d < n_line:
                    @pl.when(sends(sign, d))
                    def _():
                        hop(sign, i, c, d).start()

    for copy in local:
        copy.wait()
    for copy in pre[0]:
        copy.wait_recv()
    forward(0, 1)
    loads[1].wait()
    turn(q_in, q_turn)
    moved_q = [move(0, q_turn, q_all, 0, 0)]
    for c in range(1, chunks):
        moved[c] += move(2, v_ref, v_all, HALO, c)
        moved[c] += move(1, k_turn, k_all, HALO, c)
        moved_q.append(move(0, q_turn, q_all, 0, c))
    for c in range(chunks):
        q_all[c][own_row, :] = q_turn[:, columns(member, c)]
        k_all[c][own_kv, :] = k_turn[:, columns(member, c)]

    halos = [
        [
            pltpu.make_async_remote_copy(
                src_ref=ref[c].at[pl.ds(part * tok, HALO), :],
                dst_ref=ref[c].at[pl.ds(0, HALO), :],
                send_sem=halo_s.at[i, c], recv_sem=halo_r.at[i, c],
                device_id={"blk": (line + 1) % n_line * part + member}, device_id_type=MESH,
            )
            for i, ref in enumerate((k_all, v_all))
        ]
        for c in range(chunks)
    ]

    def send_halo(c):
        for copy in moved[c]:
            copy.wait_recv()

        @pl.when(line < n_line - 1)
        def _():
            for copy in halos[c]:
                copy.start()

        @pl.when(line == 0)
        def _():
            k_all[c][pl.ds(0, HALO), :] = jnp.zeros((HALO, some), jnp.bfloat16)
            v_all[c][pl.ds(0, HALO), :] = jnp.zeros((HALO, some), jnp.bfloat16)

    def arrive(c):
        for copy in moved_q[c]:
            copy.wait_recv()

        @pl.when(line > 0)
        def _():
            for copy in halos[c]:
                copy.wait_recv()

    def table(b, carry):
        queries = (line * part + b) * tok + lax.broadcasted_iota(jnp.int32, (tok, 1), 0)
        near = (line * part + b) * tok - HALO + lax.broadcasted_iota(jnp.int32, (1, span), 1)
        _, begins, owners, nears = lax.fori_loop(
            0, requests, lambda r, state: request(r, state, queries, near),
            (jnp.int32(0), zero, zero, jnp.zeros((1, span), jnp.int32)),
        )
        row = pl.ds(pl.multiple_of(b * tok, 16), tok)
        begin[row, :] = begins
        group_of[row, :] = owners
        near_begin[b] = nears
        return carry

    factor = math.log2(math.e) / math.sqrt(HD)
    later = lax.broadcasted_iota(jnp.int32, (tok, span), 1) - HALO <= lax.broadcasted_iota(
        jnp.int32, (tok, span), 0
    )

    def send_back(c, step):
        peer = (member + step) % part
        row = pl.ds(pl.multiple_of(peer * tok, 16), tok)
        return pltpu.make_async_remote_copy(
            src_ref=sent[c].at[row, :],
            dst_ref=attn[c].at[:, pl.ds(pl.multiple_of(member * some, some), some)],
            send_sem=back_s.at[c, step], recv_sem=back_r.at[c, step],
            device_id={"blk": base + peer}, device_id_type=MESH,
        )

    def block(c, step, carry):
        b = (member + step) % part
        row = pl.ds(pl.multiple_of(b * tok, 16), tok)
        window = pl.ds(pl.multiple_of(b * tok, 16), span)
        group = group_of[row, :]
        allowed = (near_begin[b] == begin[row, :]) & later
        for h in range(some // HD):
            at = slice(h * HD, (h + 1) * HD)
            q = q_all[c][row, at]
            near = jnp.where(allowed, dot_t(q, k_all[c][window, at]), -1e30)
            far = dot_t(q, pk_all[c][0:prefix_len, at])
            for g in range(1, GROUPS):
                far = jnp.where(
                    group == g, dot_t(q, pk_all[c][g * prefix_len:(g + 1) * prefix_len, at]), far
                )
            top = jnp.maximum(
                jnp.max(near, axis=1, keepdims=True), jnp.max(far, axis=1, keepdims=True)
            )
            e_near = jnp.exp2((near - top) * factor)
            e_far = jnp.exp2((far - top) * factor)
            total = jnp.sum(e_near, axis=1, keepdims=True) + jnp.sum(e_far, axis=1, keepdims=True)
            acc = jnp.dot(
                e_near.astype(jnp.bfloat16), v_all[c][window, at], preferred_element_type=jnp.float32
            )
            for g in range(GROUPS):
                acc += jnp.dot(
                    jnp.where(group == g, e_far, 0.0).astype(jnp.bfloat16),
                    pv_all[c][g * prefix_len:(g + 1) * prefix_len, at],
                    preferred_element_type=jnp.float32,
                )
            sent[c][row, at] = (acc / total).astype(jnp.bfloat16)

        @pl.when(step < part)
        def _():
            send_back(c, step).start()

        return carry

    def attend(c):
        lax.fori_loop(1, part + 1, functools.partial(block, c), 0)
        attn[c][:, pl.ds(pl.multiple_of(member * some, some), some)] = sent[c][own_row, :]

    def returned(c):
        for step in range(1, part):
            send_back(c, step).wait_recv()
        for copy in fetch[c * part:(c + 1) * part]:
            copy.wait()

    def project(c, at):
        return jnp.dot(attn[c][...], weight[c][:, at], preferred_element_type=jnp.float32)

    def tile(first, t):
        return pl.ds(pl.multiple_of(first + t * TILE, TILE), TILE)

    def gather(c):
        if c == 0:
            forward(0, 2)
        if c + 1 < chunks:
            for copy in pre[c + 1]:
                copy.wait_recv()
            forward(c + 1, 1)
        if c == 0:
            send_halo(0)
            lax.fori_loop(0, part, table, 0)
        for d in range(3, n_line + 1):
            forward(c, d)
        if c + 1 < chunks:
            forward(c + 1, 2)
            send_halo(c + 1)

    gather(0)
    arrive(0)
    attend(0)
    for c in range(1, chunks):
        gather(c)
        returned(c - 1)

        @pl.loop(0, n_heads * out_w // TILE)
        def _(t):
            at = tile(0, t)
            if c == 1:
                acc[:, at] = project(c - 1, at)
            else:
                acc[:, at] += project(c - 1, at)

        arrive(c)
        attend(c)
    returned(chunks - 1)

    def final(at):
        value = project(chunks - 1, at)
        return value + acc[:, at] if chunks > 1 else value

    sums = []
    for j in range(1, n_heads):
        peer = (head + j) % n_heads

        @pl.loop(0, out_w // TILE)
        def _(t):
            give[j - 1, :, tile(0, t)] = final(tile(peer * out_w, t)).astype(jnp.bfloat16)

        copy = pltpu.make_async_remote_copy(
            src_ref=give.at[j - 1], dst_ref=take.at[j - 1],
            send_sem=sum_s.at[j], recv_sem=sum_r.at[j],
            device_id={"heads": peer}, device_id_type=MESH,
        )
        copy.start()
        sums.append(copy)

    @pl.loop(0, out_w // TILE)
    def _(t):
        own[:, tile(0, t)] = final(tile(head * out_w, t)).astype(jnp.bfloat16)

    for copy in sums:
        copy.wait_recv()

    for copy in sum(pre + moved + moved_q, []) + sums:
        copy.wait_send()
    for c in range(chunks):
        for d in range(1, n_line):
            for i in range(2):
                for sign in (1, -1):
                    @pl.when(sends(sign, d))
                    def _():
                        hop(sign, i, c, d).wait_send()

        for step in range(1, part):
            send_back(c, step).wait_send()

        @pl.when(line < n_line - 1)
        def _():
            for copy in halos[c]:
                copy.wait_send()


def body(queries, keys, values, prefix_keys, prefix_values, lengths, groups, out_weight):
    tok, width = queries.shape
    rows_pre = prefix_keys.shape[0]
    n_blk = lax.axis_size("blk")
    n_heads = lax.axis_size("heads")
    part = math.gcd(4, math.gcd(width // HD, n_blk))
    n_line = n_blk // part
    cols = width // part
    chunks = math.gcd(2, cols // HD)
    some = cols // chunks
    n_pre = rows_pre * n_blk
    out_w = out_weight.shape[1] // n_heads
    vmem = pl.BlockSpec(memory_space=pltpu.VMEM)
    smem = pl.BlockSpec(memory_space=pltpu.SMEM)
    bf = jnp.bfloat16
    dma = pltpu.SemaphoreType.DMA
    own, others = pl.pallas_call(
        functools.partial(kernel, part, n_line, n_heads),
        out_shape=(
            jax.ShapeDtypeStruct((tok, out_w), bf),
            jax.ShapeDtypeStruct((n_heads - 1, tok, out_w), bf),
        ),
        in_specs=[smem, smem, vmem] + [pl.BlockSpec(memory_space=pl.ANY)] * 6,
        out_specs=(vmem, vmem),
        scratch_shapes=[
            pltpu.VMEM((tok, width), bf),
            pltpu.VMEM((tok, width), bf),
            pltpu.VMEM((tok, width), bf),
            pltpu.VMEM((tok, width), bf),
            [pltpu.VMEM((part * tok, some), bf)] * chunks,
            [pltpu.VMEM((HALO + part * tok, some), bf)] * chunks,
            [pltpu.VMEM((HALO + part * tok, some), bf)] * chunks,
            [pltpu.VMEM((n_pre, some), bf)] * chunks,
            [pltpu.VMEM((n_pre, some), bf)] * chunks,
            [pltpu.VMEM((part * tok, some), bf)] * chunks,
            [pltpu.VMEM((tok, width // chunks), bf)] * chunks,
            [pltpu.VMEM((width // chunks, out_weight.shape[1]), bf)] * chunks,
            pltpu.VMEM((n_heads - 1, tok, out_w), bf),
            pltpu.VMEM((tok, out_weight.shape[1]), jnp.float32),
            pltpu.VMEM((part * tok, 1), jnp.int32),
            pltpu.VMEM((part * tok, 1), jnp.int32),
            pltpu.VMEM((part, 1, HALO + tok), jnp.int32),
            dma((2, chunks, part)), dma((2, chunks, part)),
            dma((3, chunks, part)), dma((3, chunks, part)),
            dma((2, 2, chunks, n_line)), dma((2, 2, chunks, n_line)),
            dma((2, chunks)), dma((2, chunks)),
            dma((chunks, part)), dma((chunks, part)),
            dma((n_heads,)), dma((n_heads,)),
            dma((2,)), dma((3, chunks)), dma((chunks, part)),
        ],
        compiler_params=pltpu.CompilerParams(
            collective_id=0, has_side_effects=True, vmem_limit_bytes=56 << 20
        ),
    )(
        lengths, groups, jnp.asarray(rotary_rates()),
        queries, keys, values, prefix_keys, prefix_values, out_weight,
    )
    total = own.astype(jnp.float32)
    for j in range(n_heads - 1):
        total += others[j].astype(jnp.float32)
    return total.astype(bf)


def solution(mesh):
    placed = (
        P("blk", "heads"),
        P("blk", "heads"),
        P("blk", "heads"),
        P("blk", "heads"),
        P("blk", "heads"),
        P(),
        P(),
        P("heads", None),
    )
    return jax.shard_map(
        body, mesh=mesh, in_specs=placed, out_specs=P("blk", "heads"), check_vma=False
    )
```
